32 devices in a mesh: gx: 4 (over x, core), gy: 4 (over z), gz: 2 (over y).
Axes of the slice: x: 2, y: 2, z: 4, core: 2. Of those that a mesh axis runs over, the one named last changes fastest.
Arguments:
- positions: float32 [3, 16384], P(None, ('gx', 'gy', 'gz')), may hold values from 0 to 4, as said below
- velocities: float32 [3, 16384], P(None, ('gx', 'gy', 'gz')), may hold values from -3 to 3
- star_mass: float32 [16384], P(('gx', 'gy', 'gz')), may hold values from 0.0009765625 to 0.00390625
- far_previous: float32 [3, 16384], P(None, ('gx', 'gy', 'gz')), may hold values from -6 to 6
- cell_index: int32 [16384], P(('gx', 'gy', 'gz')), may hold values from 0 to 15, as said below
- ghost_list: int32 [8192], P(('gx', 'gy', 'gz')), may hold values from 0 to 511, as said below
- block_index: int32 [512, 128], P(('gx', 'gy', 'gz')), may hold values from 0 to 7423, as said below
- block_owner: int32 [512, 1], P(('gx', 'gy', 'gz')), may hold values from 0 to 1; in each aligned block of 16 rows (0 to 15, 16 to 31, ...) at most 16 rows name the same one
- substeps: int32 [512], P(('gx', 'gy', 'gz')), may hold values from 1 to 8, as said below
Outputs:
- far_acc: float32 [3, 16384], P(None, ('gx', 'gy', 'gz'))
- block_state: float32 [6, 131072], P(None, ('gx', 'gy', 'gz'))
The draws below stay inside these ranges and needn't reach their ends.
Inputs may be any that keep to these rules, and one draw needn't show every extreme that they name: `positions`: stars of the domain with coordinates (a, b, c) lie inside the unit box whose lowest corner is (a, b, c). `cell_index`: each cell of a domain is a box of a regular split of the domain's box, and holds at least 16 of its stars. `ghost_list`: A domain's 256 entries are distinct. `block_index`: each block's 128 entries are distinct pool columns of stars around one of the domain's own stars; no entry is a column of the domain's own sent stars or of a domain outside the grid. `block_owner`: no more than 16 of one domain's blocks have the same owner; in every draw some domain gives exactly 16 blocks to one owner. Every domain has a block with 8 substeps.
All inputs are finite; a program needn't handle non-finite values.
Results may differ from the reference program's by a relative error of at most 0.0003.
Values sent between devices are 32-bit elements; how exact they have to be, the bound alone decides.
A program may use at most 64 MiB of HBM per device.

```python
import math
import jax
import jax.numpy as jnp
import numpy as np
from jax import lax

STAR_DEV = 512
CELLS = 16
GHOSTS = 256
BLOCK = 128
BLOCKS_DEV = 16
SUBMAX = 8
DOM_X = 4
DOM_Y = 4
DOM_Z = 2
DOMAINS = 32
STARS = 16384
CAP = 16
POOL = 7424
GHOST_ROWS = 8192
BLOCK_ROWS = 512
OUT_COLS = 131072
N_GZ = 2


grid_steps = 40


def cell_splits():
    power = int(CELLS).bit_length() - 1
    return (2 ** ((power + 2) // 3), 2 ** ((power + 1) // 3), 2 ** (power // 3))


def domain_coords():
    number = jnp.arange(DOMAINS, dtype=jnp.int32)
    return jnp.stack([number // (DOM_Y * DOM_Z), number // DOM_Z % DOM_Y, number % DOM_Z], axis=1).astype(jnp.int32)


def star_layout(key):
    keys = jax.random.split(jax.random.fold_in(key, 7101), 3)
    along_x, along_y, along_z = cell_splits()
    span = jnp.array([grid_steps // along_x, grid_steps // along_y, grid_steps // along_z], jnp.int32)
    home = jnp.arange(STAR_DEV, dtype=jnp.int32) % CELLS
    lower = jnp.stack([home // (along_y * along_z), home // along_z % along_y, home % along_z], axis=1) * span[None, :]
    anywhere = jax.random.randint(keys[0], (DOMAINS, STAR_DEV, 3), 0, grid_steps).astype(jnp.int32)
    inside = jax.random.randint(keys[1], (DOMAINS, STAR_DEV, 3), 0, grid_steps).astype(jnp.int32)
    placed = lower[None] + inside % span[None, None, :]
    first = (jnp.arange(STAR_DEV, dtype=jnp.int32) < STAR_DEV // 2)[None, :, None]
    mixed = jnp.where(first, placed, anywhere)
    order = jax.vmap(lambda single: jax.random.permutation(single, STAR_DEV))(jax.random.split(keys[2], DOMAINS))
    grid_point = jnp.take_along_axis(mixed, order[:, :, None].astype(jnp.int32), axis=1).astype(jnp.int32)
    scaled = grid_point // span[None, None, :]
    cells = scaled[:, :, 0] * (along_y * along_z) + scaled[:, :, 1] * along_z + scaled[:, :, 2]
    return (grid_point, cells.astype(jnp.int32))


def ghost_layout(key):
    grid_point, cells = star_layout(key)
    keys = jax.random.split(jax.random.fold_in(key, 7102), 2)
    edge = jnp.min(jnp.minimum(grid_point, grid_steps - 1 - grid_point), axis=2)
    ties = jax.vmap(lambda single: jax.random.permutation(single, STAR_DEV))(jax.random.split(keys[0], DOMAINS)).astype(jnp.int32)
    ranked = jnp.argsort(edge * STAR_DEV + ties, axis=1)[:, :GHOSTS].astype(jnp.int32)
    shuffle = jax.vmap(lambda single: jax.random.permutation(single, GHOSTS))(jax.random.split(keys[1], DOMAINS)).astype(jnp.int32)
    listed = jnp.take_along_axis(ranked, shuffle, axis=1)
    corner = jnp.argmin(jnp.sum(grid_point, axis=2) * STAR_DEV + ties, axis=1).astype(jnp.int32)
    column = jnp.arange(GHOSTS, dtype=jnp.int32)[None, :]
    found = jnp.min(jnp.where(listed == corner[:, None], column, GHOSTS - 1), axis=1)
    last = listed[:, GHOSTS - 1]
    listed = jnp.where(column == found[:, None], last[:, None], listed)
    listed = jnp.where(column == GHOSTS - 1, corner[:, None], listed)
    return (grid_point, listed.astype(jnp.int32))


def draw_cell_index(key, part):
    grid_point, cells = star_layout(key)
    return cells.reshape(STARS).astype(jnp.int32)


def draw_ghost_list(key, part):
    grid_point, listed = ghost_layout(key)
    return listed.reshape(GHOST_ROWS).astype(jnp.int32)


def draw_positions(key, part):
    grid_point, cells = star_layout(key)
    coords = domain_coords()
    whole = (grid_point + coords[:, None, :] * grid_steps).astype(jnp.float32)
    jitter_key = jax.random.fold_in(key, 7104)
    jitter = jnp.clip(0.2 * jax.random.normal(jitter_key, (DOMAINS, STAR_DEV, 3), jnp.float32), -0.45, 0.45)
    points = (whole + 0.5 + jitter) / float(grid_steps)
    return points.transpose(2, 0, 1).reshape(3, STARS).astype(jnp.float32)


def draw_block_index(key, part):
    grid_point, listed = ghost_layout(key)
    keys = jax.random.split(jax.random.fold_in(key, 7103), 3)
    coords = domain_coords()
    global_point = (grid_point + coords[:, None, :] * grid_steps).astype(jnp.int32)
    ghost_point = jnp.take_along_axis(global_point, listed[:, :, None], axis=1)
    padded = jnp.pad(ghost_point.reshape(DOM_X, DOM_Y, DOM_Z, GHOSTS, 3), ((1, 1), (1, 1), (1, 1), (0, 0), (0, 0)))
    present = jnp.pad(jnp.ones((DOM_X, DOM_Y, DOM_Z), jnp.int32), 1)
    middle_mark = (jnp.arange(27, dtype=jnp.int32) == 13).astype(jnp.int32).reshape(3, 3, 3)
    star_number = jnp.arange(STAR_DEV, dtype=jnp.int32)
    sums = jnp.sum(grid_point, axis=2) * STAR_DEV + star_number[None, :]
    upper = jnp.argmax(sums, axis=1).astype(jnp.int32)
    lower = jnp.argmin(sums, axis=1).astype(jnp.int32)
    random_centre = jax.random.randint(keys[0], (DOMAINS, BLOCKS_DEV), 0, STAR_DEV).astype(jnp.int32)
    slot = jnp.arange(BLOCKS_DEV, dtype=jnp.int32)[None, :]
    centres = jnp.where(slot == 0, 0, random_centre)
    centres = jnp.where(slot == 1, upper[:, None], centres)
    centres = jnp.where(slot == 2, lower[:, None], centres).astype(jnp.int32)
    limit = 3 * (3 * grid_steps) ** 2 + 1
    pool_number = jnp.arange(POOL, dtype=jnp.int32)
    forced = (jnp.arange(DOMAINS, dtype=jnp.int32)[:, None] == 0) & (slot == 1)
    tie_keys = jax.random.split(keys[1], DOMAINS)
    order_keys = jax.random.split(keys[2], DOMAINS)

    def one_domain(inputs):
        number, own, centre, force_row, tie_key, order_key = inputs
        first = number // (DOM_Y * DOM_Z)
        second = number // DOM_Z % DOM_Y
        third = number % DOM_Z
        nought = jnp.zeros((), jnp.int32)
        near = lax.dynamic_slice(padded, (first, second, third, nought, nought), (3, 3, 3, GHOSTS, 3)).reshape(27 * GHOSTS, 3)
        alive = lax.dynamic_slice(present, (first, second, third), (3, 3, 3)) * (1 - middle_mark)
        alive = jnp.broadcast_to(alive.reshape(27, 1), (27, GHOSTS)).reshape(27 * GHOSTS)
        pool_point = jnp.concatenate([own, near], axis=0)
        pool_live = jnp.concatenate([jnp.ones((STAR_DEV,), jnp.int32), alive])
        middle = own[centre]
        offset = pool_point[None, :, :] - middle[:, None, :]
        distance = jnp.sum(offset * offset, axis=2)
        distance = jnp.where(pool_live[None, :] > 0, distance, limit)
        distance = jnp.where(force_row[:, None] & (pool_number[None, :] == POOL - 1), 0, distance)
        ties = jax.vmap(lambda single: jax.random.permutation(single, POOL))(jax.random.split(tie_key, BLOCKS_DEV)).astype(jnp.int32)
        nearest = jnp.argsort(distance * POOL + ties, axis=1)[:, :BLOCK].astype(jnp.int32)
        shuffle = jax.vmap(lambda single: jax.random.permutation(single, BLOCK))(jax.random.split(order_key, BLOCKS_DEV)).astype(jnp.int32)
        return jnp.take_along_axis(nearest, shuffle, axis=1).astype(jnp.int32)
    numbers = jnp.arange(DOMAINS, dtype=jnp.int32)
    chosen = lax.map(one_domain, (numbers, global_point, centres, forced, tie_keys, order_keys))
    return chosen.reshape(BLOCK_ROWS, BLOCK).astype(jnp.int32)


def draw_substeps(key, part):
    base = jax.random.fold_in(key, 7003)
    keys = jax.random.split(base, 2)
    counts = jax.random.randint(keys[0], (DOMAINS, BLOCKS_DEV), 1, SUBMAX + 1)
    chosen = jax.random.randint(keys[1], (DOMAINS, 1), 0, BLOCKS_DEV)
    counts = jnp.where(jnp.arange(BLOCKS_DEV)[None, :] == chosen, SUBMAX, counts)
    return counts.reshape(BLOCK_ROWS).astype(jnp.int32)


def block_levels(rng, extent, cuts, smallest, top_value):
    gain = 1.0
    for axis_at, parts in cuts:
        steps = jax.random.uniform(jax.random.fold_in(jax.random.fold_in(rng, 6), axis_at), (parts,), jnp.float32, smallest / len(cuts), top_value / len(cuts))
        gain = gain * jnp.repeat(jnp.exp(steps), extent[axis_at] // parts).reshape((-1,) + (1,) * (len(extent) - 1 - axis_at))
    return gain


def assign_block(key, own, number, rows, count, top, most, slope):
    ranking = jax.random.permutation(key, count)
    crowded, usual = shares(count, rows * top, most, slope, True), shares(count, rows * top, most, slope, False)
    places = jnp.arange(count)

    def named(lengths, offset_by):
        used = int((lengths > 0).sum())
        fixed = max(1, used // 4)
        passed = fixed + (places - fixed + offset_by * (used - fixed)) % max(1, count - fixed)
        return jnp.zeros((count,), jnp.int32).at[ranking[jnp.where(places < fixed, places, passed)]].set(jnp.asarray(lengths, jnp.int32))

    lengths = jnp.where(number % 4 == 0, named(crowded, number // 4), named(usual, number - number // 4 - 1))
    mixed = jax.random.permutation(jax.random.fold_in(own, 3), count)
    donor, sink = mixed[0:count // 2 * 2:2], mixed[1:count // 2 * 2:2]
    room = jnp.minimum(lengths[donor] - 1, most - lengths[sink]) // 2
    room = jnp.where((donor == ranking[0]) | (sink == ranking[0]) | (lengths[sink] == 0), 0, jnp.maximum(room, 0))
    passed = jax.random.randint(jax.random.fold_in(own, 4), (count // 2,), 0, 1 << 20) % (room + 1)
    lengths = lengths.at[donor].add(-passed).at[sink].add(passed)
    items = jnp.searchsorted(jnp.cumsum(lengths), jnp.arange(rows * top), side="right").astype(jnp.int32)
    listing = items.reshape(top, rows).T
    listing = listing[jax.random.permutation(jax.random.fold_in(own, 1), rows)]
    offset_by = jax.random.randint(jax.random.fold_in(own, 2), (rows, 1), 0, top)
    return jnp.take_along_axis(listing, (jnp.arange(top)[None, :] + offset_by) % top, axis=1)


def shares(amount, total, reach, lean, full):
    loads = [(1 << 20) // math.isqrt(standing ** lean) + 1 for standing in range(1, amount + 1)]
    largest = reach if full else min(reach, max(-(-total // amount), total * loads[0] // sum(loads)))
    least = 1 if total - largest >= amount - 1 else 0
    holding, rest = [largest] + [least] * (amount - 1), total - largest - least * (amount - 1)
    while rest > 0:
        candidates = [i for i in range(1, amount) if holding[i] < largest] or [i for i in range(1, amount) if holding[i] < reach]
        whole, left = sum([loads[i] for i in candidates]), rest
        for i in candidates:
            addition = min(reach - holding[i], max(1, left * loads[i] // whole), rest)
            holding[i] = holding[i] + addition
            rest = rest - addition
    return np.array(holding)


def scatter_about(stream_key, shape, deviation, reach, pieces=(), kind=jnp.bfloat16):
    result = deviation * jax.random.normal(stream_key, shape, jnp.float32)
    if pieces:
        result = result * block_levels(stream_key, shape, pieces, -0.22, 0.18)
    return jnp.clip(result, -reach, reach).astype(kind)


def setup_inputs(seed: int = 0) -> dict:
    arg_keys = jax.random.split(jax.random.key(seed), 10)
    positions = draw_positions(jax.random.fold_in(arg_keys[9], 71), 0)
    velocities = scatter_about(arg_keys[1], (3, STARS), 0.5, 3.0, ((1, 32),), jnp.float32)
    star_mass = jnp.clip(jnp.exp(math.log(0.00390625) - 1.3862944 * jax.random.uniform(arg_keys[2], (STARS,), jnp.float32) ** block_levels(arg_keys[2], (STARS,), ((0, 32),), -0.2, 0.2)), 0.0009765625, 0.00390625)
    far_previous = scatter_about(arg_keys[3], (3, STARS), 1.0, 6.0, ((1, 32),), jnp.float32)
    cell_index = draw_cell_index(jax.random.fold_in(arg_keys[9], 71), 0)
    ghost_list = draw_ghost_list(jax.random.fold_in(arg_keys[9], 71), 0)
    block_index = draw_block_index(jax.random.fold_in(arg_keys[9], 71), 0)
    block_owner_keys = jax.random.split(jax.random.fold_in(arg_keys[7], 1), BLOCK_ROWS // BLOCKS_DEV)
    block_owner_turns = jax.random.permutation(jax.random.fold_in(arg_keys[7], 3), BLOCK_ROWS // BLOCKS_DEV)
    block_owner = jax.vmap(lambda own, number: assign_block(jax.random.fold_in(arg_keys[7], 2), own, number, BLOCKS_DEV, N_GZ, 1, CAP, 2))(block_owner_keys, block_owner_turns).reshape((BLOCK_ROWS, 1))
    substeps = draw_substeps(jax.random.fold_in(arg_keys[9], 71), 0)
    return {"positions": positions, "velocities": velocities, "star_mass": star_mass, "far_previous": far_previous, "cell_index": cell_index, "ghost_list": ghost_list, "block_index": block_index, "block_owner": block_owner, "substeps": substeps}


SOFTENING = 0.0025
INNER_RADIUS = 0.25
OUTER_RADIUS = 1.0
TIME_STEP = 0.25

def changeover(radius):
    fraction = jnp.clip((radius - INNER_RADIUS) / (OUTER_RADIUS - INNER_RADIUS), 0.0, 1.0)
    return 1.0 - fraction * fraction * (3.0 - 2.0 * fraction)

def evaluate(position, velocity, masses):
    offset = position[:, :, None, :] - position[:, :, :, None]
    relative = velocity[:, :, None, :] - velocity[:, :, :, None]
    square = lax.optimization_barrier(jnp.sum(offset * offset, axis=0)) + SOFTENING
    radius = jnp.sqrt(square)
    weight = masses[:, None, :] * changeover(radius) / (square * radius)
    radial_rate = lax.optimization_barrier(jnp.sum(offset * relative, axis=0)) / square
    acceleration = lax.optimization_barrier(jnp.sum(weight[None] * offset, axis=-1))
    jerk_term = lax.optimization_barrier(jnp.sum(weight[None] * (relative - 3.0 * radial_rate[None] * offset), axis=-1))
    return (acceleration, jerk_term)

def integrate(state, step_count):
    start_position = state[0:3]
    start_velocity = state[3:6]
    position = start_position
    velocity = start_velocity
    masses = state[6]
    widths = (TIME_STEP / jnp.maximum(step_count, 1.0))[None, :, None]
    squared = widths * widths
    acc_old, jerk_old = evaluate(position, velocity, masses)
    for number in range(SUBMAX):
        live = (step_count > number)[None, :, None]
        predicted = position + widths * velocity + 0.5 * squared * acc_old + squared * widths / 6.0 * jerk_old
        predicted_vel = velocity + widths * acc_old + 0.5 * squared * jerk_old
        acc_new, jerk_new = evaluate(predicted, predicted_vel, masses)
        velocity_new = velocity + 0.5 * widths * (acc_old + acc_new) + squared / 12.0 * (jerk_old - jerk_new)
        position_new = position + 0.5 * widths * (velocity + velocity_new) + squared / 12.0 * (acc_old - acc_new)
        position = jnp.where(live, position_new, position)
        velocity = jnp.where(live, velocity_new, velocity)
        acc_old = jnp.where(live, acc_new, acc_old)
        jerk_old = jnp.where(live, jerk_new, jerk_old)
    return jnp.concatenate([position - start_position, velocity - start_velocity], axis=0)

def far_block(total, cells, stars):
    offset = cells[1:4, :, None] - stars[:, None, :]
    square = lax.optimization_barrier(jnp.sum(offset * offset, axis=0)) + SOFTENING
    radius = jnp.sqrt(square)
    weight = cells[0][:, None] * (1.0 - changeover(radius)) / (square * radius)
    return total + lax.optimization_barrier(jnp.sum(weight[None] * offset, axis=1))

def far_field(stars, cells):
    width = math.gcd(cells.shape[1], 512)
    blocks = cells.reshape(4, cells.shape[1] // width, width).transpose(1, 0, 2)

    def step(carry, piece):
        return (far_block(carry, piece, stars), None)
    total, unused = lax.scan(step, jnp.zeros_like(stars), blocks)
    return total

def reference(positions, velocities, star_mass, far_previous, cell_index, ghost_list, block_index, block_owner, substeps):
    star_number = jnp.arange(STARS, dtype=jnp.int32)
    segment = cell_index + star_number // STAR_DEV * CELLS
    cell_mass = jax.ops.segment_sum(star_mass, segment, DOMAINS * CELLS)
    weighted = jax.ops.segment_sum((positions * star_mass[None]).T, segment, DOMAINS * CELLS).T
    cells = jnp.concatenate([cell_mass[None], weighted / cell_mass[None]], axis=0)
    star_blocks = positions.reshape(3, DOMAINS, STAR_DEV).transpose(1, 0, 2)
    far_acc = lax.map(lambda stars: far_field(stars, cells), star_blocks)
    far_acc = far_acc.transpose(1, 0, 2).reshape(3, STARS)
    kicked = velocities + far_previous * (0.5 * TIME_STEP)
    local_rows = jnp.concatenate([positions, kicked, star_mass[None]], axis=0)
    local_rows = local_rows.reshape(7, DOMAINS, STAR_DEV).transpose(1, 0, 2)
    ghosts = jax.vmap(lambda rows, chosen: rows[:, chosen])(local_rows, ghost_list.reshape(DOMAINS, GHOSTS))
    grid = ghosts.reshape(DOM_X, DOM_Y, DOM_Z, 7, GHOSTS)
    padded = jnp.pad(grid, ((1, 1), (1, 1), (1, 1), (0, 0), (0, 0)))
    chosen_rows = block_index.reshape(DOMAINS, BLOCKS_DEV, BLOCK)
    counts = substeps.reshape(DOMAINS, BLOCKS_DEV).astype(jnp.float32)

    def one_domain(inputs):
        number, rows, chosen, step_count = inputs
        first = number // (DOM_Y * DOM_Z)
        second = number // DOM_Z % DOM_Y
        third = number % DOM_Z
        nought = jnp.zeros((), jnp.int32)
        near = lax.dynamic_slice(padded, (first, second, third, nought, nought), (3, 3, 3, 7, GHOSTS))
        near = near.transpose(3, 0, 1, 2, 4).reshape(7, 27 * GHOSTS)
        pool = jnp.concatenate([rows, near], axis=1)
        return integrate(pool[:, chosen], step_count)
    numbers = jnp.arange(DOMAINS, dtype=jnp.int32)
    results = lax.map(one_domain, (numbers, local_rows, chosen_rows, counts))
    owners = block_owner.reshape(DOMAINS, BLOCKS_DEV)
    marks = (owners[:, :, None] == jnp.arange(DOM_Z, dtype=jnp.int32)[None, None, :]).astype(jnp.int32)
    ranks = lax.optimization_barrier(jnp.sum((jnp.cumsum(marks, axis=1) - marks) * marks, axis=2))
    target = numbers[:, None] // DOM_Z * DOM_Z + owners
    source = jnp.broadcast_to(numbers[:, None] % DOM_Z, owners.shape)
    placed = jnp.zeros((DOMAINS, DOM_Z, CAP, 6, BLOCK), results.dtype)
    placed = placed.at[target, source, ranks].set(results.transpose(0, 2, 1, 3))
    block_state = placed.transpose(3, 0, 1, 2, 4).reshape(6, OUT_COLS)
    return (far_acc, block_state)
```

```python
import functools

import jax
import jax.numpy as jnp
from jax import lax
from jax.experimental import pallas as pl
from jax.experimental.pallas import tpu as pltpu
from jax.sharding import PartitionSpec as P

CELLS = 16
BLOCKS_DEV = 16
SUBMAX = 8
TOGETHER = 8
AXES = ("gx", "gy", "gz")
MESH = pl.DeviceIdType.MESH
LANES = 128

SOFTENING = 0.0025
INNER_RADIUS = 0.25
OUTER_RADIUS = 1.0
TIME_STEP = 0.25
SPAN = OUTER_RADIUS - INNER_RADIUS
CUBIC = 2.0 / SPAN**3

BF16 = jnp.bfloat16
F32 = jnp.float32
I32 = jnp.int32


def iota(shape, axis):
    return lax.broadcasted_iota(I32, shape, axis)


def halves(value):
    high = value.astype(BF16).astype(F32)
    return high, value - high


def three(value):
    high, rest = halves(value)
    middle, low = halves(rest)
    return high, middle, low


def own_rows(position, kicked, mass):
    return jnp.concatenate([position, mass, kicked, jnp.zeros_like(mass)], axis=0)


def moments(position, mass, cell):
    stars = mass.shape[1]
    number = iota((LANES, stars), 0)
    member = jnp.where(jnp.broadcast_to(cell, (LANES, stars)) == number, 1.0, 0.0).astype(BF16)
    weighted = jnp.concatenate([mass, position * mass, jnp.zeros((4, stars), F32)], axis=0)
    parts = jnp.concatenate([*three(weighted), jnp.zeros_like(weighted)], axis=0).astype(BF16)
    sums = lax.dot_general(parts, member, (((1,), (1,)), ((), ())), preferred_element_type=F32)
    sums = sums[0:8] + sums[8:16] + sums[16:24]
    inside = iota((1, LANES), 1) < CELLS
    total = jnp.where(inside, sums[0:1], 0.0)
    packed = total
    for axis in range(3):
        centre = jnp.where(inside, sums[axis + 1 : axis + 2] / jnp.where(inside, total, 1.0), 0.0)
        packed = packed + pltpu.roll(centre, (axis + 1) * CELLS, 1)
    return packed


def far_left(cells):
    high, low = halves(cells)
    fourth = iota(cells.shape, 0) == 3
    ones = [jnp.where(fourth, 1.0, part) for part in (high, low)]
    return jnp.concatenate([high, low, *ones], axis=0).astype(BF16)


def far_right(stars):
    high, low = halves(stars)
    fourth = iota(stars.shape, 0) == 3
    scaled = [jnp.where(fourth, 1.0, high * -2.0), jnp.where(fourth, 1.0, high * -2.0)]
    scaled += [jnp.where(fourth, part, low * -2.0) for part in (low, high)]
    return jnp.concatenate(scaled, axis=0).astype(BF16)


def with_norm(point, extra):
    norm = jnp.sum(point * point, axis=0, keepdims=True) + extra
    return jnp.concatenate([point, norm], axis=0)


def arrange(capacity, counts, owners, index):
    blocks, length = index.shape
    shape = (blocks, blocks)
    row, column = iota(shape, 0), iota(shape, 1)

    def across(value):
        along = jnp.broadcast_to(value.astype(F32), shape)
        return along, jnp.sum(jnp.where(row == column, along, 0.0), axis=1, keepdims=True)

    count_row, count_col = across(counts)
    owner_row, owner_col = across(owners)
    before = (count_col > count_row) | ((count_col == count_row) & (row < column))
    place = jnp.sum(jnp.where(before, 1.0, 0.0), axis=0, keepdims=True)
    turn = jnp.where(place == row.astype(F32), 1.0, 0.0).astype(BF16)
    rank = jnp.sum(jnp.where((owner_row == owner_col) & (column < row), 1.0, 0.0), axis=1, keepdims=True)
    slot = owner_col * capacity + rank
    at = iota((blocks, LANES), 1)
    facts = jnp.where(at == 0, count_col, jnp.where(at == 1, slot, 0.0))
    table = jnp.concatenate([(index & (LANES - 1)).astype(F32), (index >> 7).astype(F32), facts], axis=1)
    table = jnp.dot(turn, table.astype(BF16), preferred_element_type=F32)
    lane, chunk = table[:, 0:length].astype(I32), table[:, length : 2 * length].astype(I32)
    facts = table[:, 2 * length :]
    going = jnp.sum(jnp.where(facts[:, 0:1] > at.astype(F32), 1.0, 0.0), axis=0, keepdims=True)
    going = jnp.where(going > 0.0, jnp.maximum(going, float(TOGETHER)), 0.0)
    items = jnp.sum(going, axis=1, keepdims=True)
    going = jnp.where(iota((1, LANES), 1) == LANES - 1, items, going)
    plan = jnp.concatenate([facts, jnp.broadcast_to(going, (8, LANES))], axis=0).astype(I32)
    return lane, chunk, plan


def exchange(
    sizes, capacity,
    pos_hbm, vel_hbm, mass_hbm, far_hbm, cell_hbm, ghost_hbm, index_hbm, owner_hbm, steps_hbm,
    member_ref, plan_ref, star_ref, right_ref, every_ref,
    pos_ref, vel_ref, mass_ref, prev_ref, cell_ref, ghost_ref, index_ref, owner_ref, count_ref,
    near_ref, sent_ref, where_ref, in_sems, moment_sems, send_sems, recv_sems,
):
    domains = sizes[0] * sizes[1] * sizes[2]
    blocks = index_ref.shape[0]
    here = tuple(lax.axis_index(axis) for axis in AXES)
    loads = [
        pltpu.make_async_copy(source, into, in_sems.at[number])
        for number, (source, into) in enumerate(
            (
                (pos_hbm, pos_ref), (vel_hbm, vel_ref), (mass_hbm, mass_ref), (far_hbm, prev_ref), (cell_hbm, cell_ref),
                (ghost_hbm, ghost_ref), (index_hbm, index_ref), (owner_hbm, owner_ref), (steps_hbm, count_ref),
            )
        )
    ]
    for load in loads:
        load.start()
    barrier = pltpu.get_barrier_semaphore()

    turned = [[lax.rem(at + k, size) for k in range(size)] for at, size in zip(here[:2], sizes)]
    few = sizes[2] <= 4

    def each(act):
        for x, at_x in enumerate(turned[0]):
            for y, at_y in enumerate(turned[1]):
                first = 1 if x == 0 and y == 0 else 0

                def one(z, carry):
                    act((x * sizes[1] + y) * sizes[2] + z, (at_x, at_y, lax.rem(here[2] + z, sizes[2])))
                    return carry

                if few:
                    for z in range(first, sizes[2]):
                        one(z, 0)
                else:
                    lax.fori_loop(first, sizes[2], one, 0)

    each(lambda slot, device: pl.semaphore_signal(barrier, inc=1, device_id=device, device_id_type=MESH))
    for load in loads:
        load.wait()

    stars = pos_ref.shape[1]
    position, mass = pos_ref[...], mass_ref[...]
    kicked = vel_ref[...] + prev_ref[...] * (0.5 * TIME_STEP)
    rows = own_rows(position, kicked, mass)
    own = [rows[:, n * LANES : (n + 1) * LANES] for n in range(stars // LANES)]
    per = ghost_ref.shape[1] // LANES
    for number in range(per):
        index = jnp.broadcast_to(ghost_ref[:, number * LANES : (number + 1) * LANES], (8, LANES))
        at, part = index & (LANES - 1), index >> 7
        found = jnp.zeros((8, LANES), F32)
        for n, piece in enumerate(own):
            found = jnp.where(part == n, jnp.take_along_axis(piece, at, axis=1), found)
        sent_ref[number] = found
    every_ref[0] = moments(position, mass, cell_ref[...])

    middle = [at.astype(F32) + 0.5 for at in here]
    shift = jnp.where(
        iota((3, stars), 0) == 0, middle[0], jnp.where(iota((3, stars), 0) == 1, middle[1], middle[2])
    )
    star = with_norm(position - shift, 0.0)
    star_ref[...] = star
    right_ref[...] = far_right(star)

    lane, chunk, plan = arrange(capacity, count_ref[...], owner_ref[...], index_ref[...])
    plan_ref[...] = plan
    where_ref[0] = lane
    where_ref[1] = chunk

    def gather(pieces, first):
        for start in range(0, blocks, 8):
            names = range(start, min(start + 8, blocks))
            lanes = [jnp.broadcast_to(where_ref[0, b : b + 1, :], (8, LANES)) for b in names]
            chunks = [jnp.broadcast_to(where_ref[1, b : b + 1, :], (8, LANES)) for b in names]
            held = [jnp.zeros((8, LANES), F32) if first else member_ref[b] for b in names]
            for number, read in pieces:
                piece = read()
                held = [
                    jnp.where(c == number, jnp.take_along_axis(piece, l, axis=1), old)
                    for c, l, old in zip(chunks, lanes, held)
                ]
            for b, value in zip(names, held):
                member_ref[b] = value

    gather([(n, lambda piece=piece: piece) for n, piece in enumerate(own)], True)
    pl.semaphore_wait(barrier, domains - 1)

    def around(number):
        offset = (number // 9 - 1, number // 3 % 3 - 1, number % 3 - 1)
        there = tuple(a + b for a, b in zip(here, offset))
        inside = functools.reduce(jnp.logical_and, [(a >= 0) & (a < size) for a, size in zip(there, sizes)])
        return there, inside

    for number in range(27):
        if number != 13:
            there, inside = around(number)

            @pl.when(inside)
            def _():
                pltpu.make_async_remote_copy(
                    src_ref=sent_ref,
                    dst_ref=near_ref.at[26 - number],
                    send_sem=send_sems.at[number],
                    recv_sem=recv_sems.at[26 - number],
                    device_id=there,
                    device_id_type=MESH,
                ).start()

    def share(slot, device):
        pltpu.make_async_remote_copy(
            src_ref=every_ref.at[0],
            dst_ref=every_ref.at[slot],
            send_sem=moment_sems.at[0],
            recv_sem=moment_sems.at[1],
            device_id=device,
            device_id_type=MESH,
        ).start()

    each(share)

    def settle(number):
        there, inside = around(number)

        @pl.when(inside)
        def _():
            pltpu.make_async_copy(near_ref.at[number], near_ref.at[number], recv_sems.at[number]).wait()

    def reads(slot):
        return [
            (len(own) + slot * per + part, lambda part=part: near_ref[slot, part]) for part in range(per)
        ]

    low = jnp.where(here[2] > 0, 0, 1)
    for x in (1, 0, 2):
        for number in range(x * 9, x * 9 + 9):
            if number != 13:
                settle(number)
        pieces = []
        for y in range(3):
            at = x * 9 + y * 3
            if sizes[2] != 2:
                slots = [at + z for z in range(3) if at + z != 13]
            elif at == 12:
                slots = [at + 2 * low]
            else:
                slots = [at + low, at + low + 1]
            for slot in slots:
                pieces += reads(slot)
        gather(pieces, False)

    rest = every_ref.at[pl.ds(1, domains - 1)]
    pltpu.make_async_copy(rest, rest, moment_sems.at[0]).wait()
    pltpu.make_async_copy(rest, rest, moment_sems.at[1]).wait()
    for number in range(27):
        if number != 13:
            there, inside = around(number)

            @pl.when(inside)
            def _():
                pltpu.make_async_copy(sent_ref, sent_ref, send_sems.at[number]).wait()


class Rows:
    def __init__(self):
        row = iota((8, LANES), 0)
        self.upper = row < 4
        self.third = row == 3
        self.seventh = row == 7
        self.spare = self.third | self.seventh
        self.used = jnp.where(self.spare, 0.0, 1.0)
        self.first_used = jnp.where(row < 3, 1.0, 0.0)
        self.last_used = jnp.where(self.upper | self.spare, 0.0, 1.0)
        self.soften = jnp.where(self.third, 0.5 * SOFTENING, 0.0)
        self.double = self.first_used * -2.0
        self.turn = -self.used
        self.thrice = self.last_used * 3.0


def forces(rows, state, mass):
    swapped = pltpu.roll(state, 4, 0)
    product = state * jnp.where(rows.upper, state, swapped)
    norms = pltpu.roll(product, 1, 0) + pltpu.roll(product, 2, 0) + pltpu.roll(product, 3, 0) + rows.soften
    high, low = halves(jnp.where(rows.spare, norms, state))
    left = [high, low, jnp.where(rows.spare, 1.0, high), jnp.where(rows.spare, 1.0, low)]

    def right(one, high_part, low_part):
        lead = jnp.where(one, 1.0, high_part)
        return [lead, lead, jnp.where(one, low, low_part), jnp.where(one, high, low_part)]

    square_side = right(rows.third, high * rows.double, low * rows.double)
    rate_side = right(rows.seventh, pltpu.roll(high, 4, 0) * rows.turn, pltpu.roll(low, 4, 0) * rows.turn)
    pairs = lax.dot_general(
        jnp.concatenate(left, axis=0).astype(BF16),
        jnp.concatenate(
            [jnp.concatenate(square_side, axis=0).astype(BF16), jnp.concatenate(rate_side, axis=0).astype(BF16)], axis=1
        ),
        (((0,), (0,)), ((), ())),
        preferred_element_type=F32,
    )
    square, rate = pairs[:, 0:LANES], pairs[:, LANES:]
    inverse = lax.rsqrt(square)
    inverse2 = inverse * inverse
    near = jnp.clip(OUTER_RADIUS - square * inverse, 0.0, SPAN)
    weight = (near * near) * (1.5 * SPAN - near) * (inverse * inverse2)
    turned = weight * (rate * inverse2)
    matrix = []
    for value in (weight, turned):
        high_part = value.astype(BF16)
        matrix.append(jnp.concatenate([high_part, (value - high_part.astype(F32)).astype(BF16)], axis=0))
    matrix = jnp.concatenate(matrix, axis=1)
    values = jnp.concatenate(halves(jnp.where(rows.third, 1.0, state) * mass), axis=0).astype(BF16)
    sums = jnp.dot(jnp.concatenate([values, values], axis=1), matrix, preferred_element_type=F32)
    sums = sums[0:8] + sums[8:16]
    plain, bent = sums[:, 0:LANES], sums[:, LANES:]
    straight = plain - state * jnp.broadcast_to(plain[3:4], (8, LANES))
    curved = bent - state * jnp.broadcast_to(bent[3:4], (8, LANES))
    return straight - rows.thrice * pltpu.roll(curved, 4, 0)


def step_stars(
    plan_vmem, member_ref, out_ref, plan_ref, state_ref, force_ref, mass_ref, origin_ref, sem,
):
    blocks = member_ref.shape[0]
    fetch = pltpu.make_async_copy(plan_vmem, plan_ref, sem)
    fetch.start()
    out_ref[...] = jnp.zeros_like(out_ref)
    rows = Rows()

    def begin(number, carry):
        for g in range(TOGETHER):
            name = number * TOGETHER + g
            value = member_ref[name]
            middle = jnp.sum(value, axis=1, keepdims=True) * (1.0 / LANES)
            middle = jnp.broadcast_to(middle, (8, LANES))
            state = (value - middle) * rows.used
            mass = jnp.broadcast_to(value[3:4], (8, LANES)) * CUBIC
            state_ref[name] = state
            mass_ref[name] = mass
            origin_ref[name] = state - rows.first_used * pltpu.roll(middle, 4, 0) * TIME_STEP
            force_ref[name] = forces(rows, state, mass)
        return carry

    lax.fori_loop(0, blocks // TOGETHER, begin, 0)
    fetch.wait()

    def advance(number, carry):
        step, place = carry
        limit = plan_ref[blocks, step]
        names, widths = [], []
        for g in range(TOGETHER):
            over = place + g >= limit
            name = jnp.where(over, place + g - limit, place + g)
            count = plan_ref[name, 0]
            live = count > step + over.astype(I32)
            names.append(name)
            widths.append(jnp.where(live, TIME_STEP / count.astype(F32), 0.0))
        fresh = []
        for name, width in zip(names, widths):
            state, force, mass = state_ref[name], force_ref[name], mass_ref[name]
            h = rows.used * width
            squared = h * h
            moving = h * jnp.where(rows.upper, pltpu.roll(state, 4, 0), pltpu.roll(force, 4, 0))
            cubed = squared * h * (rows.first_used * (1.0 / 6.0))
            predicted = state + moving + (0.5 * squared) * force + cubed * pltpu.roll(force, 4, 0)
            force_new = forces(rows, predicted, mass)
            gap = force - force_new
            half = 0.5 * h
            change = moving + squared * (1.0 / 12.0) * gap - half * rows.last_used * pltpu.roll(gap, 4, 0)
            change = change + half * rows.first_used * pltpu.roll(change, 4, 0)
            fresh.append((name, state + change, force_new))
        for name, state, force in fresh:
            state_ref[name] = state
            force_ref[name] = force
        place = place + TOGETHER
        over = place >= limit
        return jnp.where(over, step + 1, step), jnp.where(over, place - limit, place)

    items = plan_ref[blocks, LANES - 1]
    lax.fori_loop(0, (items + (TOGETHER - 1)) // TOGETHER, advance, (jnp.int32(0), jnp.int32(0)))
    for name in range(blocks):
        change = state_ref[name] - origin_ref[name]
        at = pl.multiple_of(plan_ref[name, 1] * LANES, LANES)
        out_ref[:, pl.ds(at, LANES)] = jnp.concatenate([change[0:3], change[4:7]], axis=0)


def far_field(here, star_ref, right_ref, every_ref, far_ref):
    stars = star_ref.shape[1]
    domains = every_ref.shape[0]
    row, column = iota((8, LANES), 0), iota((8, LANES), 1)
    middle = [at.astype(F32) + 0.5 for at in here]
    shift = jnp.where(row == 6, middle[0], jnp.where(row == 5, middle[1], jnp.where(row == 4, middle[2], 0.0)))

    def some(number, total):
        table = every_ref[pl.ds(pl.multiple_of(number * 8, 8), 8), :]
        cells = jnp.zeros((8, LANES), F32)
        for j in range(8):
            spread = jnp.broadcast_to(table[j : j + 1], (8, LANES))
            spread = pltpu.roll(pltpu.roll(spread, CELLS * ((j + 1) % 8), 1), 0, 1, stride=CELLS, stride_axis=0)
            cells = jnp.where(column // CELLS == j, spread, cells)
        cells = cells - shift
        mass = cells[7:8] * CUBIC
        centre = jnp.concatenate([cells[6:7], cells[5:6], cells[4:5]], axis=0)
        left = far_left(with_norm(centre, SOFTENING))
        square = lax.dot_general(left, right_ref[...], (((0,), (0,)), ((), ())), preferred_element_type=F32)
        inverse = lax.rsqrt(square)
        gone = jnp.clip(square * inverse - INNER_RADIUS, 0.0, SPAN)
        weight = (gone * gone) * (1.5 * SPAN - gone) * (inverse * inverse * inverse)
        high = weight.astype(BF16)
        matrix = jnp.concatenate([high, (weight - high.astype(F32)).astype(BF16)], axis=0)
        values = jnp.concatenate([centre * mass, mass, jnp.zeros((4, LANES), F32)], axis=0)
        values = jnp.concatenate(halves(values), axis=0).astype(BF16)
        sums = jnp.dot(jnp.concatenate([values, values], axis=1), matrix, preferred_element_type=F32)
        return total + sums[0:8] + sums[8:16]

    total = lax.fori_loop(0, domains // 8, some, jnp.zeros((8, stars), F32))
    far_ref[...] = total[0:3] - star_ref[0:3, :] * total[3:4]


def deliver(lanes, packed_ref, star_ref, right_ref, every_ref, out_ref, far_ref, own_sem, sems):
    here = tuple(lax.axis_index(axis) for axis in AXES)
    me = here[2]
    part = packed_ref.shape[1] // lanes
    barrier = pltpu.get_barrier_semaphore()

    def columns(number):
        return pl.ds(pl.multiple_of(number * part, LANES), part)

    def other(step):
        there = lax.rem(me + step, lanes)
        return there, (here[0], here[1], there)

    def greet(step, carry):
        pl.semaphore_signal(barrier, inc=1, device_id=other(step)[1], device_id_type=MESH)
        return carry

    lax.fori_loop(1, lanes, greet, 0)
    own = pltpu.make_async_copy(packed_ref.at[:, columns(me)], out_ref.at[:, columns(me)], own_sem)
    own.start()
    pl.semaphore_wait(barrier, lanes - 1)

    def send(step, carry):
        there, device = other(step)
        pltpu.make_async_remote_copy(
            src_ref=packed_ref.at[:, columns(there)],
            dst_ref=out_ref.at[:, columns(me)],
            send_sem=sems.at[0],
            recv_sem=sems.at[1],
            device_id=device,
            device_id_type=MESH,
        ).start()
        return carry

    lax.fori_loop(1, lanes, send, 0)
    far_field(here, star_ref, right_ref, every_ref, far_ref)
    own.wait()
    rest = packed_ref.at[:, pl.ds(0, (lanes - 1) * part)]
    pltpu.make_async_copy(rest, rest, sems.at[0]).wait()
    pltpu.make_async_copy(rest, rest, sems.at[1]).wait()


def finish(far_ref, arrived_ref, far_out_ref, out_ref, sems):
    first = pltpu.make_async_copy(arrived_ref, out_ref, sems.at[0])
    second = pltpu.make_async_copy(far_ref, far_out_ref, sems.at[1])
    first.start()
    second.start()
    first.wait()
    second.wait()


def vmem(count):
    return [pl.BlockSpec(memory_space=pltpu.VMEM)] * count


def hbm(count):
    return [pl.BlockSpec(memory_space=pltpu.HBM)] * count


def params(**more):
    return pltpu.CompilerParams(vmem_limit_bytes=16 * 1024 * 1024, **more)


def on_device(
    sizes, positions, velocities, star_mass, far_previous, cell_index, ghost_list, block_index, block_owner, substeps
):
    lanes = sizes[2]
    domains = sizes[0] * sizes[1] * sizes[2]
    blocks, length = block_index.shape
    capacity = max(2, 2 * BLOCKS_DEV // lanes)
    stars, ghosts = positions.shape[1], ghost_list.shape[0]
    shape = jax.ShapeDtypeStruct
    sent = (ghosts // LANES, 8, LANES)
    member, plan, star, right, every = pl.pallas_call(
        functools.partial(exchange, sizes, capacity),
        out_shape=(
            shape((blocks, 8, LANES), F32),
            shape((blocks + 8, LANES), I32),
            shape((4, stars), F32),
            shape((16, stars), BF16),
            shape((domains, 1, LANES), F32),
        ),
        in_specs=hbm(9),
        out_specs=tuple(vmem(5)),
        scratch_shapes=[
            pltpu.VMEM((3, stars), F32),
            pltpu.VMEM((3, stars), F32),
            pltpu.VMEM((1, stars), F32),
            pltpu.VMEM((3, stars), F32),
            pltpu.VMEM((1, stars), I32),
            pltpu.VMEM((1, ghosts), I32),
            pltpu.VMEM((blocks, length), I32),
            pltpu.VMEM((1, blocks), I32),
            pltpu.VMEM((1, blocks), I32),
            pltpu.VMEM((27, *sent), F32),
            pltpu.VMEM(sent, F32),
            pltpu.VMEM((2, blocks, length), I32),
            pltpu.SemaphoreType.DMA((9,)),
            pltpu.SemaphoreType.DMA((2,)),
            pltpu.SemaphoreType.DMA((27,)),
            pltpu.SemaphoreType.DMA((27,)),
        ],
        compiler_params=params(collective_id=0, has_side_effects=True),
        name="exchange",
    )(
        *(
            pltpu.with_memory_space_constraint(array, pltpu.HBM)
            for array in (
                positions,
                velocities,
                star_mass.reshape(1, stars),
                far_previous,
                cell_index.reshape(1, stars),
                ghost_list.reshape(1, ghosts),
                block_index,
                block_owner.reshape(1, blocks),
                substeps.reshape(1, blocks),
            )
        )
    )
    block = pltpu.VMEM((blocks, 8, LANES), F32)
    packed = pl.pallas_call(
        step_stars,
        out_shape=shape((6, lanes * capacity * length), F32),
        in_specs=vmem(2),
        out_specs=vmem(1)[0],
        scratch_shapes=[pltpu.SMEM(plan.shape, I32), block, block, block, block, pltpu.SemaphoreType.DMA],
        compiler_params=params(),
        name="step_stars",
    )(plan, member)
    arrived, far_acc = pl.pallas_call(
        functools.partial(deliver, lanes),
        out_shape=(shape(packed.shape, F32), shape((3, stars), F32)),
        in_specs=vmem(4),
        out_specs=tuple(vmem(2)),
        scratch_shapes=[pltpu.SemaphoreType.DMA, pltpu.SemaphoreType.DMA((2,))],
        compiler_params=params(collective_id=1, has_side_effects=True),
        name="deliver",
    )(packed, star, right, every.reshape(domains, LANES))
    return pl.pallas_call(
        finish,
        out_shape=(shape(far_acc.shape, F32), shape(arrived.shape, F32)),
        in_specs=vmem(2),
        out_specs=tuple(hbm(2)),
        scratch_shapes=[pltpu.SemaphoreType.DMA((2,))],
        compiler_params=params(),
        name="finish",
    )(far_acc, arrived)


def solution(mesh):
    split = P(AXES)
    wide = P(None, AXES)
    tall = P(AXES, None)
    return jax.shard_map(
        functools.partial(on_device, tuple(mesh.shape[axis] for axis in AXES)),
        mesh=mesh,
        in_specs=(wide, wide, split, wide, split, split, tall, tall, split),
        out_specs=(wide, wide),
        check_vma=False,
    )
```

```python
import functools

import jax
import jax.numpy as jnp
from jax import lax
from jax.experimental import pallas as pl
from jax.experimental.pallas import tpu as pltpu
from jax.sharding import PartitionSpec as P

CELLS = 16
BLOCKS_DEV = 16
SUBMAX = 8
TOGETHER = 8
AXES = ("gx", "gy", "gz")
MESH = pl.DeviceIdType.MESH
LANES = 128

SOFTENING = 0.0025
INNER_RADIUS = 0.25
OUTER_RADIUS = 1.0
TIME_STEP = 0.25
SPAN = OUTER_RADIUS - INNER_RADIUS
CUBIC = 2.0 / SPAN**3

BF16 = jnp.bfloat16
F32 = jnp.float32
I32 = jnp.int32


def iota(shape, axis):
    return lax.broadcasted_iota(I32, shape, axis)


def halves(value):
    high = value.astype(BF16).astype(F32)
    return high, value - high


def three(value):
    high, rest = halves(value)
    middle, low = halves(rest)
    return high, middle, low


def own_rows(position, kicked, mass):
    return jnp.concatenate([position, mass, kicked, jnp.zeros_like(mass)], axis=0)


def moments(position, mass, cell):
    stars = mass.shape[1]
    number = iota((LANES, stars), 0)
    member = jnp.where(jnp.broadcast_to(cell, (LANES, stars)) == number, 1.0, 0.0).astype(BF16)
    weighted = jnp.concatenate([mass, position * mass, jnp.zeros((4, stars), F32)], axis=0)
    parts = jnp.concatenate([*three(weighted), jnp.zeros_like(weighted)], axis=0).astype(BF16)
    sums = lax.dot_general(parts, member, (((1,), (1,)), ((), ())), preferred_element_type=F32)
    sums = sums[0:8] + sums[8:16] + sums[16:24]
    inside = iota((1, LANES), 1) < CELLS
    total = jnp.where(inside, sums[0:1], 0.0)
    packed = total
    for axis in range(3):
        centre = jnp.where(inside, sums[axis + 1 : axis + 2] / jnp.where(inside, total, 1.0), 0.0)
        packed = packed + pltpu.roll(centre, (axis + 1) * CELLS, 1)
    return packed


def far_left(cells):
    high, low = halves(cells)
    fourth = iota(cells.shape, 0) == 3
    ones = [jnp.where(fourth, 1.0, part) for part in (high, low)]
    return jnp.concatenate([high, low, *ones], axis=0).astype(BF16)


def far_right(stars):
    high, low = halves(stars)
    fourth = iota(stars.shape, 0) == 3
    scaled = [jnp.where(fourth, 1.0, high * -2.0), jnp.where(fourth, 1.0, high * -2.0)]
    scaled += [jnp.where(fourth, part, low * -2.0) for part in (low, high)]
    return jnp.concatenate(scaled, axis=0).astype(BF16)


def with_norm(point, extra):
    norm = jnp.sum(point * point, axis=0, keepdims=True) + extra
    return jnp.concatenate([point, norm], axis=0)


def arrange(capacity, counts, owners, index):
    blocks, length = index.shape
    shape = (blocks, blocks)
    row, column = iota(shape, 0), iota(shape, 1)

    def across(value):
        along = jnp.broadcast_to(value.astype(F32), shape)
        return along, jnp.sum(jnp.where(row == column, along, 0.0), axis=1, keepdims=True)

    count_row, count_col = across(counts)
    owner_row, owner_col = across(owners)
    before = (count_col > count_row) | ((count_col == count_row) & (row < column))
    place = jnp.sum(jnp.where(before, 1.0, 0.0), axis=0, keepdims=True)
    turn = jnp.where(place == row.astype(F32), 1.0, 0.0).astype(BF16)
    rank = jnp.sum(jnp.where((owner_row == owner_col) & (column < row), 1.0, 0.0), axis=1, keepdims=True)
    slot = owner_col * capacity + rank
    at = iota((blocks, LANES), 1)
    facts = jnp.where(at == 0, count_col, jnp.where(at == 1, slot, 0.0))
    table = jnp.concatenate([(index & (LANES - 1)).astype(F32), (index >> 7).astype(F32), facts], axis=1)
    table = jnp.dot(turn, table.astype(BF16), preferred_element_type=F32)
    lane, chunk = table[:, 0:length].astype(I32), table[:, length : 2 * length].astype(I32)
    facts = table[:, 2 * length :]
    going = jnp.sum(jnp.where(facts[:, 0:1] > at.astype(F32), 1.0, 0.0), axis=0, keepdims=True)
    going = jnp.where(going > 0.0, jnp.maximum(going, float(TOGETHER)), 0.0)
    items = jnp.sum(going, axis=1, keepdims=True)
    going = jnp.where(iota((1, LANES), 1) == LANES - 1, items, going)
    plan = jnp.concatenate([facts, jnp.broadcast_to(going, (8, LANES))], axis=0).astype(I32)
    return lane, chunk, plan


def exchange(
    sizes, capacity,
    pos_hbm, vel_hbm, mass_hbm, far_hbm, cell_hbm, ghost_hbm, index_hbm, owner_hbm, steps_hbm,
    member_ref, plan_ref, star_ref, right_ref, every_ref,
    pos_ref, vel_ref, mass_ref, prev_ref, cell_ref, ghost_ref, index_ref, owner_ref, count_ref,
    near_ref, sent_ref, where_ref, in_sems, moment_sems, send_sems, recv_sems,
):
    domains = sizes[0] * sizes[1] * sizes[2]
    blocks = index_ref.shape[0]
    here = tuple(lax.axis_index(axis) for axis in AXES)
    loads = [
        pltpu.make_async_copy(source, into, in_sems.at[number])
        for number, (source, into) in enumerate(
            (
                (pos_hbm, pos_ref), (vel_hbm, vel_ref), (mass_hbm, mass_ref), (far_hbm, prev_ref), (cell_hbm, cell_ref),
                (ghost_hbm, ghost_ref), (index_hbm, index_ref), (owner_hbm, owner_ref), (steps_hbm, count_ref),
            )
        )
    ]
    for load in loads:
        load.start()
    barrier = pltpu.get_barrier_semaphore()

    outward = here[1] * 2 < sizes[1]
    steps_y = [jnp.where(outward, sizes[1] - k, k) if k else jnp.int32(0) for k in range(sizes[1])]
    turned_x = [lax.rem(here[0] + k, sizes[0]) for k in range(sizes[0])]
    turned_y = [lax.rem(here[1] + k, sizes[1]) for k in steps_y]
    few = sizes[2] <= 4

    def each(act):
        for y in (*range(1, sizes[1]), 0):
            for x in reversed(range(sizes[0])):
                first = 1 if x == 0 and y == 0 else 0

                def one(z, carry):
                    slot = (x * sizes[1] + steps_y[y]) * sizes[2] + z
                    act(slot, (turned_x[x], turned_y[y], lax.rem(here[2] + z, sizes[2])))
                    return carry

                if few:
                    for z in reversed(range(first, sizes[2])):
                        one(z, 0)
                else:
                    lax.fori_loop(first, sizes[2], one, 0)

    each(lambda slot, device: pl.semaphore_signal(barrier, inc=1, device_id=device, device_id_type=MESH))
    for load in loads:
        load.wait()

    stars = pos_ref.shape[1]
    position, mass = pos_ref[...], mass_ref[...]
    kicked = vel_ref[...] + prev_ref[...] * (0.5 * TIME_STEP)
    rows = own_rows(position, kicked, mass)
    own = [rows[:, n * LANES : (n + 1) * LANES] for n in range(stars // LANES)]
    per = ghost_ref.shape[1] // LANES
    for number in range(per):
        index = jnp.broadcast_to(ghost_ref[:, number * LANES : (number + 1) * LANES], (8, LANES))
        at, part = index & (LANES - 1), index >> 7
        found = jnp.zeros((8, LANES), F32)
        for n, piece in enumerate(own):
            found = jnp.where(part == n, jnp.take_along_axis(piece, at, axis=1), found)
        sent_ref[number] = found
    every_ref[0] = moments(position, mass, cell_ref[...])

    pl.semaphore_wait(barrier, domains - 1)

    def around(number):
        offset = (number // 9 - 1, number // 3 % 3 - 1, number % 3 - 1)
        there = tuple(a + b for a, b in zip(here, offset))
        inside = functools.reduce(jnp.logical_and, [(a >= 0) & (a < size) for a, size in zip(there, sizes)])
        return there, inside

    for number in range(27):
        if number != 13:
            there, inside = around(number)

            @pl.when(inside)
            def _():
                pltpu.make_async_remote_copy(
                    src_ref=sent_ref,
                    dst_ref=near_ref.at[26 - number],
                    send_sem=send_sems.at[number],
                    recv_sem=recv_sems.at[26 - number],
                    device_id=there,
                    device_id_type=MESH,
                ).start()

    def share(slot, device):
        pltpu.make_async_remote_copy(
            src_ref=every_ref.at[0],
            dst_ref=every_ref.at[slot],
            send_sem=moment_sems.at[0],
            recv_sem=moment_sems.at[1],
            device_id=device,
            device_id_type=MESH,
        ).start()

    each(share)

    middle = [at.astype(F32) + 0.5 for at in here]
    shift = jnp.where(
        iota((3, stars), 0) == 0, middle[0], jnp.where(iota((3, stars), 0) == 1, middle[1], middle[2])
    )
    star = with_norm(position - shift, 0.0)
    star_ref[...] = star
    right_ref[...] = far_right(star)

    lane, chunk, plan = arrange(capacity, count_ref[...], owner_ref[...], index_ref[...])
    plan_ref[...] = plan
    where_ref[0] = lane
    where_ref[1] = chunk

    def gather(pieces, first):
        for start in range(0, blocks, 8):
            names = range(start, min(start + 8, blocks))
            lanes = [jnp.broadcast_to(where_ref[0, b : b + 1, :], (8, LANES)) for b in names]
            chunks = [jnp.broadcast_to(where_ref[1, b : b + 1, :], (8, LANES)) for b in names]
            held = [jnp.zeros((8, LANES), F32) if first else member_ref[b] for b in names]
            for number, read in pieces:
                piece = read()
                held = [
                    jnp.where(c == number, jnp.take_along_axis(piece, l, axis=1), old)
                    for c, l, old in zip(chunks, lanes, held)
                ]
            for b, value in zip(names, held):
                member_ref[b] = value

    gather([(n, lambda piece=piece: piece) for n, piece in enumerate(own)], True)
    def settle(number):
        there, inside = around(number)

        @pl.when(inside)
        def _():
            pltpu.make_async_copy(near_ref.at[number], near_ref.at[number], recv_sems.at[number]).wait()

    def reads(slot):
        return [
            (len(own) + slot * per + part, lambda part=part: near_ref[slot, part]) for part in range(per)
        ]

    low = jnp.where(here[2] > 0, 0, 1)
    for x in (1, 0, 2):
        for number in range(x * 9, x * 9 + 9):
            if number != 13:
                settle(number)
        pieces = []
        for y in range(3):
            at = x * 9 + y * 3
            if sizes[2] != 2:
                slots = [at + z for z in range(3) if at + z != 13]
            elif at == 12:
                slots = [at + 2 * low]
            else:
                slots = [at + low, at + low + 1]
            for slot in slots:
                pieces += reads(slot)
        gather(pieces, False)

    for number in range(27):
        if number != 13:
            there, inside = around(number)

            @pl.when(inside)
            def _():
                pltpu.make_async_copy(sent_ref, sent_ref, send_sems.at[number]).wait()
    rest = every_ref.at[pl.ds(1, domains - 1)]
    pltpu.make_async_copy(rest, rest, moment_sems.at[0]).wait()
    pltpu.make_async_copy(rest, rest, moment_sems.at[1]).wait()


class Rows:
    def __init__(self):
        row = iota((8, LANES), 0)
        self.upper = row < 4
        self.third = row == 3
        self.seventh = row == 7
        self.spare = self.third | self.seventh
        self.used = jnp.where(self.spare, 0.0, 1.0)
        self.first_used = jnp.where(row < 3, 1.0, 0.0)
        self.last_used = jnp.where(self.upper | self.spare, 0.0, 1.0)
        self.soften = jnp.where(self.third, 0.5 * SOFTENING, 0.0)
        self.double = self.first_used * -2.0
        self.turn = -self.used
        self.thrice = self.last_used * 3.0


def forces(rows, state, mass):
    swapped = pltpu.roll(state, 4, 0)
    product = state * jnp.where(rows.upper, state, swapped)
    norms = pltpu.roll(product, 1, 0) + pltpu.roll(product, 2, 0) + pltpu.roll(product, 3, 0) + rows.soften
    high, low = halves(jnp.where(rows.spare, norms, state))
    left = [high, low, jnp.where(rows.spare, 1.0, high), jnp.where(rows.spare, 1.0, low)]

    def right(one, high_part, low_part):
        lead = jnp.where(one, 1.0, high_part)
        return [lead, lead, jnp.where(one, low, low_part), jnp.where(one, high, low_part)]

    square_side = right(rows.third, high * rows.double, low * rows.double)
    rate_side = right(rows.seventh, pltpu.roll(high, 4, 0) * rows.turn, pltpu.roll(low, 4, 0) * rows.turn)
    pairs = lax.dot_general(
        jnp.concatenate(left, axis=0).astype(BF16),
        jnp.concatenate(
            [jnp.concatenate(square_side, axis=0).astype(BF16), jnp.concatenate(rate_side, axis=0).astype(BF16)], axis=1
        ),
        (((0,), (0,)), ((), ())),
        preferred_element_type=F32,
    )
    square, rate = pairs[:, 0:LANES], pairs[:, LANES:]
    inverse = lax.rsqrt(square)
    inverse2 = inverse * inverse
    near = jnp.clip(OUTER_RADIUS - square * inverse, 0.0, SPAN)
    weight = (near * near) * (1.5 * SPAN - near) * (inverse * inverse2)
    turned = weight * (rate * inverse2)
    matrix = []
    for value in (weight, turned):
        high_part = value.astype(BF16)
        matrix.append(jnp.concatenate([high_part, (value - high_part.astype(F32)).astype(BF16)], axis=0))
    matrix = jnp.concatenate(matrix, axis=1)
    values = jnp.concatenate(halves(jnp.where(rows.third, 1.0, state) * mass), axis=0).astype(BF16)
    sums = jnp.dot(jnp.concatenate([values, values], axis=1), matrix, preferred_element_type=F32)
    sums = sums[0:8] + sums[8:16]
    plain, bent = sums[:, 0:LANES], sums[:, LANES:]
    straight = plain - state * jnp.broadcast_to(plain[3:4], (8, LANES))
    curved = bent - state * jnp.broadcast_to(bent[3:4], (8, LANES))
    return straight - rows.thrice * pltpu.roll(curved, 4, 0)


def step_stars(
    plan_vmem, member_ref, out_ref, plan_ref, state_ref, force_ref, mass_ref, origin_ref, scale_ref, sem,
):
    blocks = member_ref.shape[0]
    fetch = pltpu.make_async_copy(plan_vmem, plan_ref, sem)
    fetch.start()
    out_ref[...] = jnp.zeros_like(out_ref)
    rows = Rows()

    def begin(number, carry):
        for g in range(TOGETHER):
            name = number * TOGETHER + g
            value = member_ref[name]
            middle = jnp.sum(value, axis=1, keepdims=True) * (1.0 / LANES)
            middle = jnp.broadcast_to(middle, (8, LANES))
            state = (value - middle) * rows.used
            mass = jnp.broadcast_to(value[3:4], (8, LANES)) * CUBIC
            state_ref[name] = state
            mass_ref[name] = mass
            origin_ref[name] = state - rows.first_used * pltpu.roll(middle, 4, 0) * TIME_STEP
            count = jnp.broadcast_to(plan_vmem[pl.ds(name, 1), 0:1], (8, LANES)).astype(F32)
            width = TIME_STEP / jnp.maximum(count, 1.0) * rows.used
            half, squared = 0.5 * width, width * width
            for kind, scale in enumerate(
                (
                    width, 0.5 * squared, squared * width * (1.0 / 6.0) * rows.first_used, squared * (1.0 / 12.0),
                    half * rows.last_used, half * rows.first_used,
                )
            ):
                scale_ref[name, kind] = scale
            force_ref[name] = forces(rows, state, mass)
        return carry

    lax.fori_loop(0, blocks // TOGETHER, begin, 0)
    fetch.wait()

    def advance(number, carry):
        step, place = carry
        limit = plan_ref[blocks, step]
        work = []
        for g in range(TOGETHER):
            over = place + g >= limit
            name = jnp.where(over, place + g - limit, place + g)
            work.append((name, jnp.where(plan_ref[name, 0] > step + over.astype(I32), 1.0, 0.0)))
        fresh = []
        for name, live in work:
            state, force = state_ref[name], force_ref[name]
            moving = scale_ref[name, 0] * jnp.where(rows.upper, pltpu.roll(state, 4, 0), pltpu.roll(force, 4, 0))
            predicted = state + moving + scale_ref[name, 1] * force + scale_ref[name, 2] * pltpu.roll(force, 4, 0)
            force_new = forces(rows, predicted, mass_ref[name])
            gap = force - force_new
            change = moving + scale_ref[name, 3] * gap - scale_ref[name, 4] * pltpu.roll(gap, 4, 0)
            change = change + scale_ref[name, 5] * pltpu.roll(change, 4, 0)
            fresh.append((name, state + live * change, force_new))
        for name, state, force in fresh:
            state_ref[name] = state
            force_ref[name] = force
        place = place + TOGETHER
        over = place >= limit
        return jnp.where(over, step + 1, step), jnp.where(over, place - limit, place)

    items = plan_ref[blocks, LANES - 1]
    lax.fori_loop(0, (items + (TOGETHER - 1)) // TOGETHER, advance, (jnp.int32(0), jnp.int32(0)))
    for name in range(blocks):
        change = state_ref[name] - origin_ref[name]
        at = pl.multiple_of(plan_ref[name, 1] * LANES, LANES)
        out_ref[:, pl.ds(at, LANES)] = jnp.concatenate([change[0:3], change[4:7]], axis=0)


def far_field(here, star_ref, right_ref, every_ref, far_ref):
    stars = star_ref.shape[1]
    domains = every_ref.shape[0]
    row, column = iota((8, LANES), 0), iota((8, LANES), 1)
    middle = [at.astype(F32) + 0.5 for at in here]
    shift = jnp.where(row == 6, middle[0], jnp.where(row == 5, middle[1], jnp.where(row == 4, middle[2], 0.0)))

    def some(number, total):
        table = every_ref[pl.ds(pl.multiple_of(number * 8, 8), 8), :]
        cells = jnp.zeros((8, LANES), F32)
        for j in range(8):
            spread = jnp.broadcast_to(table[j : j + 1], (8, LANES))
            spread = pltpu.roll(pltpu.roll(spread, CELLS * ((j + 1) % 8), 1), 0, 1, stride=CELLS, stride_axis=0)
            cells = jnp.where(column // CELLS == j, spread, cells)
        cells = cells - shift
        mass = cells[7:8] * CUBIC
        centre = jnp.concatenate([cells[6:7], cells[5:6], cells[4:5]], axis=0)
        left = far_left(with_norm(centre, SOFTENING))
        square = lax.dot_general(left, right_ref[...], (((0,), (0,)), ((), ())), preferred_element_type=F32)
        inverse = lax.rsqrt(square)
        gone = jnp.clip(square * inverse - INNER_RADIUS, 0.0, SPAN)
        weight = (gone * gone) * (1.5 * SPAN - gone) * (inverse * inverse * inverse)
        high = weight.astype(BF16)
        matrix = jnp.concatenate([high, (weight - high.astype(F32)).astype(BF16)], axis=0)
        values = jnp.concatenate([centre * mass, mass, jnp.zeros((4, LANES), F32)], axis=0)
        values = jnp.concatenate(halves(values), axis=0).astype(BF16)
        sums = jnp.dot(jnp.concatenate([values, values], axis=1), matrix, preferred_element_type=F32)
        return total + sums[0:8] + sums[8:16]

    total = lax.fori_loop(0, domains // 8, some, jnp.zeros((8, stars), F32))
    far_ref[...] = total[0:3] - star_ref[0:3, :] * total[3:4]


def deliver(lanes, packed_ref, star_ref, right_ref, every_ref, out_ref, far_ref, own_sem, sems):
    here = tuple(lax.axis_index(axis) for axis in AXES)
    me = here[2]
    part = packed_ref.shape[1] // lanes
    barrier = pltpu.get_barrier_semaphore()

    def columns(number):
        return pl.ds(pl.multiple_of(number * part, LANES), part)

    def other(step):
        there = lax.rem(me + step, lanes)
        return there, (here[0], here[1], there)

    def greet(step, carry):
        pl.semaphore_signal(barrier, inc=1, device_id=other(step)[1], device_id_type=MESH)
        return carry

    lax.fori_loop(1, lanes, greet, 0)
    own = pltpu.make_async_copy(packed_ref.at[:, columns(me)], out_ref.at[:, columns(me)], own_sem)
    own.start()
    pl.semaphore_wait(barrier, lanes - 1)

    def send(step, carry):
        there, device = other(step)
        pltpu.make_async_remote_copy(
            src_ref=packed_ref.at[:, columns(there)],
            dst_ref=out_ref.at[:, columns(me)],
            send_sem=sems.at[0],
            recv_sem=sems.at[1],
            device_id=device,
            device_id_type=MESH,
        ).start()
        return carry

    lax.fori_loop(1, lanes, send, 0)
    far_field(here, star_ref, right_ref, every_ref, far_ref)
    own.wait()
    rest = packed_ref.at[:, pl.ds(0, (lanes - 1) * part)]
    pltpu.make_async_copy(rest, rest, sems.at[0]).wait()
    pltpu.make_async_copy(rest, rest, sems.at[1]).wait()


def finish(far_ref, arrived_ref, far_out_ref, out_ref, sems):
    first = pltpu.make_async_copy(arrived_ref, out_ref, sems.at[0])
    second = pltpu.make_async_copy(far_ref, far_out_ref, sems.at[1])
    first.start()
    second.start()
    first.wait()
    second.wait()


def vmem(count):
    return [pl.BlockSpec(memory_space=pltpu.VMEM)] * count


def hbm(count):
    return [pl.BlockSpec(memory_space=pltpu.HBM)] * count


def params(**more):
    return pltpu.CompilerParams(vmem_limit_bytes=16 * 1024 * 1024, **more)


def on_device(
    sizes, positions, velocities, star_mass, far_previous, cell_index, ghost_list, block_index, block_owner, substeps
):
    lanes = sizes[2]
    domains = sizes[0] * sizes[1] * sizes[2]
    blocks, length = block_index.shape
    capacity = max(2, 2 * BLOCKS_DEV // lanes)
    stars, ghosts = positions.shape[1], ghost_list.shape[0]
    shape = jax.ShapeDtypeStruct
    sent = (ghosts // LANES, 8, LANES)
    member, plan, star, right, every = pl.pallas_call(
        functools.partial(exchange, sizes, capacity),
        out_shape=(
            shape((blocks, 8, LANES), F32),
            shape((blocks + 8, LANES), I32),
            shape((4, stars), F32),
            shape((16, stars), BF16),
            shape((domains, 1, LANES), F32),
        ),
        in_specs=hbm(9),
        out_specs=tuple(vmem(5)),
        scratch_shapes=[
            pltpu.VMEM((3, stars), F32),
            pltpu.VMEM((3, stars), F32),
            pltpu.VMEM((1, stars), F32),
            pltpu.VMEM((3, stars), F32),
            pltpu.VMEM((1, stars), I32),
            pltpu.VMEM((1, ghosts), I32),
            pltpu.VMEM((blocks, length), I32),
            pltpu.VMEM((1, blocks), I32),
            pltpu.VMEM((1, blocks), I32),
            pltpu.VMEM((27, *sent), F32),
            pltpu.VMEM(sent, F32),
            pltpu.VMEM((2, blocks, length), I32),
            pltpu.SemaphoreType.DMA((9,)),
            pltpu.SemaphoreType.DMA((2,)),
            pltpu.SemaphoreType.DMA((27,)),
            pltpu.SemaphoreType.DMA((27,)),
        ],
        compiler_params=params(collective_id=0, has_side_effects=True),
        name="exchange",
    )(
        *(
            pltpu.with_memory_space_constraint(array, pltpu.HBM)
            for array in (
                positions,
                velocities,
                star_mass.reshape(1, stars),
                far_previous,
                cell_index.reshape(1, stars),
                ghost_list.reshape(1, ghosts),
                block_index,
                block_owner.reshape(1, blocks),
                substeps.reshape(1, blocks),
            )
        )
    )
    block = pltpu.VMEM((blocks, 8, LANES), F32)
    packed = pl.pallas_call(
        step_stars,
        out_shape=shape((6, lanes * capacity * length), F32),
        in_specs=vmem(2),
        out_specs=vmem(1)[0],
        scratch_shapes=[
            pltpu.SMEM(plan.shape, I32),
            block,
            block,
            block,
            block,
            pltpu.VMEM((blocks, 6, 8, LANES), F32),
            pltpu.SemaphoreType.DMA,
        ],
        compiler_params=params(),
        name="step_stars",
    )(plan, member)
    arrived, far_acc = pl.pallas_call(
        functools.partial(deliver, lanes),
        out_shape=(shape(packed.shape, F32), shape((3, stars), F32)),
        in_specs=vmem(4),
        out_specs=tuple(vmem(2)),
        scratch_shapes=[pltpu.SemaphoreType.DMA, pltpu.SemaphoreType.DMA((2,))],
        compiler_params=params(collective_id=1, has_side_effects=True),
        name="deliver",
    )(packed, star, right, every.reshape(domains, LANES))
    return pl.pallas_call(
        finish,
        out_shape=(shape(far_acc.shape, F32), shape(arrived.shape, F32)),
        in_specs=vmem(2),
        out_specs=tuple(hbm(2)),
        scratch_shapes=[pltpu.SemaphoreType.DMA((2,))],
        compiler_params=params(),
        name="finish",
    )(far_acc, arrived)


def solution(mesh):
    split = P(AXES)
    wide = P(None, AXES)
    tall = P(AXES, None)
    return jax.shard_map(
        functools.partial(on_device, tuple(mesh.shape[axis] for axis in AXES)),
        mesh=mesh,
        in_specs=(wide, wide, split, wide, split, split, tall, tall, split),
        out_specs=(wide, wide),
        check_vma=False,
    )
```
